32 devices in a mesh: dp: 16 (over z, y, x), tensor: 2 (over core).
Axes of the slice: x: 2, y: 2, z: 4, core: 2. Of those that a mesh axis runs over, the one named last changes fastest.
Arguments:
- grads: bfloat16 [16, 256, 3584], P('dp', None, 'tensor'), may hold values from -6 to 6
- residual: float32 [16, 256, 3584], P('dp', None, 'tensor'), may hold values from -4 to 4
- q_prev: float32 [3584, 64], P('tensor'), may hold values from -6 to 6
Outputs:
- q_next: float32 [3584, 64], P('tensor')
- basis: float32 [256, 64], replicated
- new_residual: float32 [16, 256, 3584], P('dp', None, 'tensor')
The draws below stay inside these ranges and needn't reach their ends.
All inputs are finite; a program needn't handle non-finite values.
Results may differ from the reference program's by a relative error of at most 0.0003.
Values sent between devices are 32-bit elements; how exact they have to be, the bound alone decides.
A program may use at most 64 MiB of HBM per device.

```python
import jax
import jax.numpy as jnp
from jax import lax

ROWS = 256
RANK = 64
COLS = 3584
N_DP = 16


def shard_levels(stream_key, dims, cuts, least, high):
    loudness = 1.0
    for position, blocks in cuts:
        draws = jax.random.uniform(jax.random.fold_in(jax.random.fold_in(stream_key, 6), position), (blocks,), jnp.float32, least / len(cuts), high / len(cuts))
        loudness = loudness * jnp.repeat(jnp.exp(draws), dims[position] // blocks).reshape((-1,) + (1,) * (len(dims) - 1 - position))
    return loudness


def normal_values(rng, shape, scale, bound, cuts=(), kind=jnp.bfloat16):
    values = jax.random.normal(rng, shape, jnp.float32) * scale
    if len(cuts) > 0:
        values = shard_levels(rng, shape, cuts, -0.22, 0.18) * values
    return jnp.clip(values, min=-bound, max=bound).astype(kind)


def setup_inputs(seed: int = 0) -> dict:
    seeds = jax.random.split(jax.random.key(seed), 4)
    return {
        "grads": normal_values(seeds[0], (N_DP, ROWS, COLS), 1.0, 6.0, ((0, 16), (2, 2))),
        "residual": normal_values(seeds[1], (N_DP, ROWS, COLS), 0.5, 4.0, ((0, 16), (2, 2)), jnp.float32),
        "q_prev": normal_values(seeds[2], (COLS, RANK), 1.0, 6.0, ((0, 2),), jnp.float32),
    }


def reference(grads, residual, q_prev):
    high = lax.Precision.HIGHEST
    merged = grads.astype(jnp.float32) + residual
    left = jnp.einsum('irc,ck->rk', merged, q_prev.astype(jnp.float32), precision=high) / N_DP
    gram = jnp.dot(left.T, left, precision=high)
    lower = jnp.linalg.cholesky(gram)
    basis = jax.scipy.linalg.solve_triangular(lower, left.T, lower=True).T
    q_next = jnp.einsum('irc,rk->ck', merged, basis, precision=high) / N_DP
    update = jnp.dot(basis, q_next.T, precision=high)
    new_residual = merged - update[None]
    return (q_next, basis, new_residual)
```

```python
import functools

import jax
import jax.numpy as jnp
from jax import lax
from jax.experimental import pallas as pl
from jax.experimental.pallas import tpu as pltpu
from jax.sharding import PartitionSpec as P

MESH = pl.DeviceIdType.MESH
HIGHEST = lax.Precision.HIGHEST
SUB, LANE = 8, 128


def split(x):
    hi = x.astype(jnp.bfloat16)
    lo = (x - hi.astype(jnp.float32)).astype(jnp.bfloat16)
    return hi, lo


def dot(a, b, dims=((1,), (0,)), precision=None):
    return lax.dot_general(a, b, (dims, ((), ())), precision=precision, preferred_element_type=jnp.float32)


def eliminate(tiles, start, stop, rank):
    tiles = list(tiles)
    index = lax.broadcasted_iota(jnp.int32, tiles[0].shape, 0)
    for k in range(start, stop):
        block, r = divmod(k, SUB)
        row = tiles[block][r : r + 1, :]
        scaled = row * (1.0 / row[:, k : k + 1])
        for b in range(block, rank // SUB):
            if b == block and r == SUB - 1:
                continue
            column = tiles[b][:, k : k + 1]
            if b == block:
                column = jnp.where(index[:, :1] > r, column, 0.0)
            tiles[b] = tiles[b] - column * scaled
    return tiles


def kernel(
    n, inner, outer, tensor,
    g_ref, r_ref, q_ref, new_ref, next_ref, basis_ref,
    m_hi, m_lo, left_own, left_in, left_mid, left_all,
    t_own, t_in, t_sum, t_in2, t_all, gram_b, sems_send, sems_recv,
):
    rows, cols = g_ref.shape
    rank = q_ref.shape[0]
    block = 2 * LANE
    me_dp, me_t = lax.axis_index("dp"), lax.axis_index("tensor")
    i, o = lax.rem(me_dp, inner), lax.div(me_dp, inner)
    near = inner * tensor
    place = i * tensor + me_t

    def near_device(k):
        peer = lax.rem(place + k, near)
        return peer, (o * inner + lax.div(peer, tensor), lax.rem(peer, tensor))

    def plane_device(k):
        peer = lax.rem(i + k, inner)
        return peer, (o * inner + peer, me_t)

    def far_device(k):
        peer = lax.rem(o + k, outer)
        return peer, (peer * inner + i, me_t)

    barrier = pltpu.get_barrier_semaphore()
    for k in range(1, near):
        pl.semaphore_signal(barrier, inc=1, device_id=near_device(k)[1], device_id_type=MESH)
    for k in range(1, outer):
        pl.semaphore_signal(barrier, inc=1, device_id=far_device(k)[1], device_id_type=MESH)

    used = [0]

    def send(src, dst, device):
        slot = used[0]
        used[0] += 1
        copy = pltpu.make_async_remote_copy(
            src_ref=src, dst_ref=dst, send_sem=sems_send.at[slot], recv_sem=sems_recv.at[slot],
            device_id=device, device_id_type=MESH,
        )
        copy.start()
        return copy

    sent = []

    def arrive(copies):
        for copy in copies:
            copy.wait_recv()
        sent.extend(copies)

    q_hi, q_lo = split(q_ref[...])
    q_two = jnp.concatenate([q_hi, q_lo], axis=0)
    total = jnp.zeros((2 * rank, rows), jnp.float32)
    low = jnp.zeros((rank, rows), jnp.float32)
    for c in range(0, cols, block):
        hi, lo = split(g_ref[:, c : c + block].astype(jnp.float32) + r_ref[:, c : c + block])
        m_hi[:, c : c + block] = hi
        m_lo[:, c : c + block] = lo
        total += dot(q_two[:, c : c + block], hi, ((1,), (1,)))
        low += dot(q_hi[:, c : c + block], lo, ((1,), (1,)))
    part = (total[:rank] + total[rank:]) + low
    tall = rank // SUB
    left_tiles = tall * (rows // LANE)
    for b in range(rows // LANE):
        left_own[b * tall : (b + 1) * tall] = part[:, b * LANE : (b + 1) * LANE].reshape(tall, SUB, LANE)
    if left_own.shape[0] > left_tiles:
        left_own[left_tiles:] = jnp.zeros((left_own.shape[0] - left_tiles, SUB, LANE), jnp.float32)
    piece = left_own.shape[0] // near

    pl.semaphore_wait(barrier, near - 1 + outer - 1)

    copies = []
    for k in range(1, near):
        peer, device = near_device(k)
        copies.append(send(left_own.at[pl.ds(peer * piece, piece)], left_in.at[k], device))
    arrive(copies)
    value = left_own[pl.ds(place * piece, piece)]
    for k in range(1, near):
        value += left_in[k]
    left_mid[o] = value
    copies = []
    for k in range(1, outer):
        _, device = far_device(k)
        copies.append(send(left_mid.at[o], left_mid.at[o], device))
    arrive(copies)
    value = left_mid[0]
    for k in range(1, outer):
        value += left_mid[k]
    here = left_all.at[pl.ds(place * piece, piece)]
    here[...] = value / n
    copies = []
    for k in range(1, near):
        copies.append(send(here, here, near_device(k)[1]))
    arrive(copies)
    left = jnp.concatenate(
        [left_all[b * tall : (b + 1) * tall].reshape(rank, LANE) for b in range(rows // LANE)], axis=1
    )

    l_hi, l_lo = split(left)
    l_two = jnp.concatenate([l_hi, l_lo], axis=0)
    t_tiles = tall * (cols // LANE)
    for c in range(0, cols, block):
        both = dot(l_two, m_hi[:, c : c + block])
        value = (both[:rank] + both[rank:]) + dot(l_hi, m_lo[:, c : c + block])
        for d in range(0, block, LANE):
            b = (c + d) // LANE
            t_own[b * tall : (b + 1) * tall] = value[:, d : d + LANE].reshape(tall, SUB, LANE)
    if t_own.shape[0] > t_tiles:
        t_own[t_tiles:] = jnp.zeros((t_own.shape[0] - t_tiles, SUB, LANE), jnp.float32)
    small = t_own.shape[0] // n
    large = small * outer

    copies = []
    for k in range(1, inner):
        peer, device = plane_device(k)
        copies.append(send(t_own.at[pl.ds(peer * large, large)], t_in.at[k], device))

    gram_b[:rank] = left
    gram_b[rank:] = jnp.zeros_like(left)
    gram = dot(left, gram_b[...], ((1,), (1,)), HIGHEST)
    row_id = lax.broadcasted_iota(jnp.int32, gram.shape, 0)
    lane_id = lax.broadcasted_iota(jnp.int32, gram.shape, 1)
    gram = gram + jnp.where(lane_id == row_id + rank, 1.0, 0.0)
    tiles = [gram[b : b + SUB] for b in range(0, rank, SUB)]
    tiles = eliminate(tiles, 0, rank, rank)
    done = jnp.concatenate(tiles, axis=0)
    pivot = jnp.sum(jnp.where(lane_id == row_id, done, 0.0), axis=1, keepdims=True)
    done = done * (1.0 / jnp.sqrt(pivot))
    w_two = jnp.where(lane_id < rank, pltpu.roll(done, rank, 1), done)
    basis = dot(w_two[:, :rank], left, precision=HIGHEST)
    basis_ref[...] = basis
    b_hi, b_lo = split(jnp.concatenate([basis, basis], axis=0).T)
    b_four = jnp.concatenate([b_hi, b_lo], axis=1)
    w_hi, w_lo = split(w_two / n)
    w_four = jnp.concatenate([w_hi, w_lo], axis=1)

    arrive(copies)
    mine = t_own[pl.ds(i * large, large)]
    for k in range(1, inner):
        mine += t_in[k]
    t_sum[...] = mine
    copies = []
    for k in range(1, outer):
        peer, device = far_device(k)
        copies.append(send(t_sum.at[pl.ds(peer * small, small)], t_in2.at[k], device))
    arrive(copies)
    mine = t_sum[pl.ds(o * small, small)]
    for k in range(1, outer):
        mine += t_in2[k]
    here = t_all.at[pl.ds(i * large + o * small, small)]
    here[...] = mine
    copies = []
    for k in range(1, outer):
        copies.append(send(here, here, far_device(k)[1]))
    arrive(copies)
    here = t_all.at[pl.ds(i * large, large)]
    copies = []
    for k in range(1, inner):
        copies.append(send(here, here, plane_device(k)[1]))
    arrive(copies)

    for c in range(0, cols, block):
        t = jnp.concatenate(
            [t_all[b * tall : (b + 1) * tall].reshape(rank, LANE) for b in range(c // LANE, (c + block) // LANE)],
            axis=1,
        )
        t_hi, t_lo = split(t)
        q_next = dot(w_four, jnp.concatenate([t_hi, t_lo, t_hi, t_lo], axis=0))
        next_ref[:, c : c + block] = q_next
        n_hi, n_lo = split(q_next)
        update = dot(b_four, jnp.concatenate([n_hi, n_lo, n_hi, n_lo], axis=0))
        merged = g_ref[:, c : c + block].astype(jnp.float32) + r_ref[:, c : c + block]
        new_ref[:, c : c + block] = merged - update

    for copy in sent:
        copy.wait_send()


def local(grads, residual, q_prev):
    n, tensor = lax.axis_size("dp"), lax.axis_size("tensor")
    inner = max(d for d in range(1, n + 1) if n % d == 0 and d * d <= n)
    outer = n // inner
    rows, cols = grads.shape[1:]
    rank = q_prev.shape[1]
    near = inner * tensor
    left_piece = pl.cdiv((rank // SUB) * (rows // LANE), near)
    small = pl.cdiv((rank // SUB) * (cols // LANE), n)
    copies = 2 * (near - 1) + 3 * (outer - 1) + 2 * (inner - 1)
    f32 = jnp.float32
    tile = lambda *dims: pltpu.VMEM((*dims, SUB, LANE), f32)
    vmem = pl.BlockSpec(memory_space=pltpu.VMEM)
    new, q_next, basis = pl.pallas_call(
        functools.partial(kernel, n, inner, outer, tensor),
        out_shape=(
            jax.ShapeDtypeStruct((rows, cols), f32),
            jax.ShapeDtypeStruct((rank, cols), f32),
            jax.ShapeDtypeStruct((rank, rows), f32),
        ),
        in_specs=[vmem] * 3,
        out_specs=(vmem,) * 3,
        scratch_shapes=[
            pltpu.VMEM((rows, cols), jnp.bfloat16),
            pltpu.VMEM((rows, cols), jnp.bfloat16),
            tile(near * left_piece),
            tile(near, left_piece),
            tile(outer, left_piece),
            tile(near * left_piece),
            tile(n * small),
            tile(inner, outer * small),
            tile(outer * small),
            tile(outer, small),
            tile(n * small),
            pltpu.VMEM((2 * rank, rows), f32),
            pltpu.SemaphoreType.DMA((copies,)),
            pltpu.SemaphoreType.DMA((copies,)),
        ],
        compiler_params=pltpu.CompilerParams(collective_id=0, has_side_effects=True),
        name="powersgd",
    )(grads[0], residual[0], q_prev.T)
    return (q_next.T, basis.T, new[None])


def solution(mesh):
    in_specs = (P("dp", None, "tensor"), P("dp", None, "tensor"), P("tensor", None))
    out_specs = (P("tensor", None), P(), P("dp", None, "tensor"))
    return jax.shard_map(local, mesh=mesh, in_specs=in_specs, out_specs=out_specs, check_vma=False)
```

```python
import functools

import jax
import jax.numpy as jnp
from jax import lax
from jax.experimental import pallas as pl
from jax.experimental.pallas import tpu as pltpu
from jax.sharding import PartitionSpec as P

MESH = pl.DeviceIdType.MESH
HIGHEST = lax.Precision.HIGHEST
SUB, LANE = 8, 128
FIRST_STEPS = 40
VMEM_LIMIT = 24 << 20


def split(x):
    hi = x.astype(jnp.bfloat16)
    lo = (x - hi.astype(jnp.float32)).astype(jnp.bfloat16)
    return hi, lo


def dot(a, b, dims=((1,), (0,)), precision=None):
    return lax.dot_general(a, b, (dims, ((), ())), precision=precision, preferred_element_type=jnp.float32)


def eliminate(tiles, start, stop, rank):
    tiles = list(tiles)
    index = lax.broadcasted_iota(jnp.int32, tiles[0].shape, 0)
    for k in range(start, stop):
        block, r = divmod(k, SUB)
        row = tiles[block][r : r + 1, :]
        scaled = row * (1.0 / row[:, k : k + 1])
        for b in range(block, rank // SUB):
            if b == block and r == SUB - 1:
                continue
            column = tiles[b][:, k : k + 1]
            if b == block:
                column = jnp.where(index[:, :1] > r, column, 0.0)
            tiles[b] = tiles[b] - column * scaled
    return tiles


def reduce_kernel(
    n, inner, outer, tensor,
    g_hbm, r_hbm, q_ref, m_ref, t_ref, b_ref, w_ref, basis_ref,
    g_in, r_in, m_hi, m_lo, left_own, left_in, left_mid, left_all,
    t_own, t_in, t_sum, t_in2, t_all, gram_b, sems_load, sems_send, sems_recv,
):
    rows, cols = g_in.shape
    rank = q_ref.shape[0]
    block = 2 * LANE
    starts = range(0, cols, block)
    loads = []
    for j, c in enumerate(starts):
        here = pl.ds(c, block)
        pair = (
            pltpu.make_async_copy(g_hbm.at[:, here], g_in.at[:, here], sems_load.at[0, j]),
            pltpu.make_async_copy(r_hbm.at[:, here], r_in.at[:, here], sems_load.at[1, j]),
        )
        for copy in pair:
            copy.start()
        loads.append(pair)

    me_dp, me_t = lax.axis_index("dp"), lax.axis_index("tensor")
    i, o = lax.rem(me_dp, inner), lax.div(me_dp, inner)
    near = inner * tensor
    place = i * tensor + me_t

    def near_device(k):
        peer = lax.rem(place + k, near)
        return peer, (o * inner + lax.div(peer, tensor), lax.rem(peer, tensor))

    def plane_device(k):
        peer = lax.rem(i + k, inner)
        return peer, (o * inner + peer, me_t)

    def far(j):
        low = jnp.where(outer - 1 - j > o, outer - 1 - j, outer - 2 - j)
        high = jnp.where(j < o, j, j + 1)
        return jnp.where(2 * o < outer, low, high)

    def far_device(peer):
        return (peer * inner + i, me_t)

    barrier = pltpu.get_barrier_semaphore()
    for k in range(1, near):
        pl.semaphore_signal(barrier, inc=1, device_id=near_device(k)[1], device_id_type=MESH)
    for k in range(1, outer):
        pl.semaphore_signal(barrier, inc=1, device_id=far_device(lax.rem(o + k, outer)), device_id_type=MESH)

    used = [0]
    sent = []

    def slots(count):
        used[0] += count
        return used[0] - count

    def remote(src, dst, slot, device):
        return pltpu.make_async_remote_copy(
            src_ref=src, dst_ref=dst, send_sem=sems_send.at[len(sent)], recv_sem=sems_recv.at[slot],
            device_id=device, device_id_type=MESH,
        )

    def send(src, dst, slot, device):
        copy = remote(src, dst, slot, device)
        copy.start()
        sent.append(copy)
        return copy

    def landed(dst, slot):
        remote(dst, dst, slot, near_device(1)[1]).wait_recv()

    q_hi, q_lo = split(q_ref[...])
    q_two = jnp.concatenate([q_hi, q_lo], axis=0)
    total = jnp.zeros((2 * rank, rows), jnp.float32)
    low = jnp.zeros((rank, rows), jnp.float32)
    for (load_g, load_r), c in zip(loads, starts):
        load_g.wait()
        load_r.wait()
        merged = g_in[:, c : c + block].astype(jnp.float32) + r_in[:, c : c + block]
        m_ref[:, c : c + block] = merged
        hi, lo = split(merged)
        m_hi[:, c : c + block] = hi
        m_lo[:, c : c + block] = lo
        total += dot(q_two[:, c : c + block], hi, ((1,), (1,)))
        low += dot(q_hi[:, c : c + block], lo, ((1,), (1,)))
    part = (total[:rank] + total[rank:]) + low
    tall = rank // SUB
    left_tiles = tall * (rows // LANE)
    for b in range(rows // LANE):
        left_own[b * tall : (b + 1) * tall] = part[:, b * LANE : (b + 1) * LANE].reshape(tall, SUB, LANE)
    if left_own.shape[0] > left_tiles:
        left_own[left_tiles:] = jnp.zeros((left_own.shape[0] - left_tiles, SUB, LANE), jnp.float32)
    piece = left_own.shape[0] // near

    pl.semaphore_wait(barrier, near - 1 + outer - 1)

    base = slots(near)
    copies = []
    for k in range(1, near):
        peer, device = near_device(k)
        copies.append(send(left_own.at[pl.ds(peer * piece, piece)], left_in.at[k], base + k, device))
    value = left_own[pl.ds(place * piece, piece)]
    for k, copy in enumerate(copies):
        copy.wait_recv()
        value += left_in[k + 1]
    left_mid[o] = value
    base = slots(outer)
    for j in range(outer - 1):
        send(left_mid.at[o], left_mid.at[o], base + o, far_device(far(j)))
    for j in reversed(range(outer - 1)):
        landed(left_mid.at[far(j)], base + far(j))
    value = left_mid[0]
    for k in range(1, outer):
        value += left_mid[k]
    here = left_all.at[pl.ds(place * piece, piece)]
    here[...] = value / n
    base = slots(near)
    copies = [send(here, here, base + k, near_device(k)[1]) for k in range(1, near)]
    for copy in copies:
        copy.wait_recv()
    left = jnp.concatenate(
        [left_all[b * tall : (b + 1) * tall].reshape(rank, LANE) for b in range(rows // LANE)], axis=1
    )

    l_hi, l_lo = split(left)
    l_two = jnp.concatenate([l_hi, l_lo], axis=0)
    t_tiles = tall * (cols // LANE)
    for c in starts:
        both = dot(l_two, m_hi[:, c : c + block])
        value = (both[:rank] + both[rank:]) + dot(l_hi, m_lo[:, c : c + block])
        for d in range(0, block, LANE):
            b = (c + d) // LANE
            t_own[b * tall : (b + 1) * tall] = value[:, d : d + LANE].reshape(tall, SUB, LANE)
    if t_own.shape[0] > t_tiles:
        t_own[t_tiles:] = jnp.zeros((t_own.shape[0] - t_tiles, SUB, LANE), jnp.float32)
    small = t_own.shape[0] // n
    large = small * outer

    order = [far(j) for j in range(outer - 1)] + [o]
    base = slots(outer * inner)
    steps = []
    for j, b in enumerate(order):
        copies = []
        for k in range(1, inner):
            peer, device = plane_device(k)
            copies.append(send(
                t_own.at[pl.ds(peer * large + b * small, small)], t_in.at[k, pl.ds(b * small, small)],
                base + j * inner + k, device,
            ))
        steps.append(copies)

    gram_b[:rank] = left
    gram_b[rank:] = jnp.zeros_like(left)
    gram = dot(left, gram_b[...], ((1,), (1,)), HIGHEST)
    row_id = lax.broadcasted_iota(jnp.int32, gram.shape, 0)
    lane_id = lax.broadcasted_iota(jnp.int32, gram.shape, 1)
    gram = gram + jnp.where(lane_id == row_id + rank, 1.0, 0.0)
    tiles = [gram[b : b + SUB] for b in range(0, rank, SUB)]
    middle = FIRST_STEPS * rank // 64
    tiles = eliminate(tiles, 0, middle, rank)

    base = slots(outer)
    for copies, b in zip(steps, order):
        mine = t_own[pl.ds(i * large + b * small, small)]
        for k, copy in enumerate(copies):
            copy.wait_recv()
            mine += t_in[k + 1, pl.ds(b * small, small)]
        there = t_sum.at[pl.ds(b * small, small)]
        there[...] = mine
        if copies is not steps[-1]:
            send(there, t_in2.at[o], base + o, far_device(b))

    tiles = eliminate(tiles, middle, rank, rank)

    mine = t_sum[pl.ds(o * small, small)]
    for b in order[:-1]:
        landed(t_in2.at[b], base + b)
        mine += t_in2[b]
    here = t_all.at[pl.ds(i * large + o * small, small)]
    here[...] = mine
    base = slots(outer)
    for b in order[:-1]:
        send(here, here, base + o, far_device(b))
    last = slots(inner * outer)

    def spread(b):
        part = t_all.at[pl.ds(i * large + b * small, small)]
        for k in range(1, inner):
            send(part, part, last + k * outer + b, plane_device(k)[1])

    spread(o)

    done = jnp.concatenate(tiles, axis=0)
    pivot = jnp.sum(jnp.where(lane_id == row_id, done, 0.0), axis=1, keepdims=True)
    done = done * (1.0 / jnp.sqrt(pivot))
    w_two = jnp.where(lane_id < rank, pltpu.roll(done, rank, 1), done)
    basis = dot(w_two[:, :rank], left, precision=HIGHEST)
    basis_ref[...] = basis
    w_hi, w_lo = split(w_two / n)
    w_ref[...] = jnp.concatenate([w_hi, w_lo], axis=1)

    for b in reversed(order[:-1]):
        landed(t_all.at[pl.ds(i * large + b * small, small)], base + b)
        spread(b)

    b_hi, b_lo = split(jnp.concatenate([basis, basis], axis=0).T)
    b_ref[...] = jnp.concatenate([b_hi, b_lo], axis=1)

    for b in range(outer):
        for k in range(1, inner):
            peer = lax.rem(i + inner - k, inner)
            landed(t_all.at[pl.ds(peer * large + b * small, small)], last + k * outer + b)
    t_ref[...] = t_all[:t_tiles]
    for copy in sent:
        copy.wait_send()


def finish_kernel(
    m_ref, t_ref, b_ref, w_ref, basis_ref, new_hbm, next_hbm, out_basis_ref,
    new_out, next_out, sems_store,
):
    rank, cols = next_out.shape
    tall = rank // SUB
    block = 2 * LANE
    out_basis_ref[...] = basis_ref[...]
    stores = []
    for j, c in enumerate(range(0, cols, block)):
        here = pl.ds(c, block)
        t = jnp.concatenate(
            [t_ref[b * tall : (b + 1) * tall].reshape(rank, LANE) for b in range(c // LANE, (c + block) // LANE)],
            axis=1,
        )
        t_hi, t_lo = split(t)
        q_next = dot(w_ref[...], jnp.concatenate([t_hi, t_lo, t_hi, t_lo], axis=0))
        next_out[:, c : c + block] = q_next
        stores.append(pltpu.make_async_copy(next_out.at[:, here], next_hbm.at[:, here], sems_store.at[0, j]))
        stores[-1].start()
        n_hi, n_lo = split(q_next)
        update = dot(b_ref[...], jnp.concatenate([n_hi, n_lo, n_hi, n_lo], axis=0))
        new_out[:, c : c + block] = m_ref[:, c : c + block] - update
        stores.append(pltpu.make_async_copy(new_out.at[:, here], new_hbm.at[:, here], sems_store.at[1, j]))
        stores[-1].start()
    for copy in stores:
        copy.wait()


def local(grads, residual, q_prev):
    n, tensor = lax.axis_size("dp"), lax.axis_size("tensor")
    inner = max(d for d in range(1, n + 1) if n % d == 0 and d * d <= n)
    outer = n // inner
    rows, cols = grads.shape[1:]
    rank = q_prev.shape[1]
    near = inner * tensor
    t_tiles = (rank // SUB) * (cols // LANE)
    left_piece = pl.cdiv((rank // SUB) * (rows // LANE), near)
    small = pl.cdiv(t_tiles, n)
    copies = 2 * near + 4 * outer + 2 * inner * outer
    f32, bf16 = jnp.float32, jnp.bfloat16
    tile = lambda *dims: pltpu.VMEM((*dims, SUB, LANE), f32)
    vmem = pl.BlockSpec(memory_space=pltpu.VMEM)
    hbm = pl.BlockSpec(memory_space=pltpu.HBM)
    chunks = cols // (2 * LANE)
    merged, t_sum, b_four, w_four, basis = pl.pallas_call(
        functools.partial(reduce_kernel, n, inner, outer, tensor),
        out_shape=(
            jax.ShapeDtypeStruct((rows, cols), f32),
            jax.ShapeDtypeStruct((t_tiles, SUB, LANE), f32),
            jax.ShapeDtypeStruct((rows, 4 * rank), bf16),
            jax.ShapeDtypeStruct((rank, 4 * rank), bf16),
            jax.ShapeDtypeStruct((rank, rows), f32),
        ),
        in_specs=[hbm, hbm, vmem],
        out_specs=(vmem,) * 5,
        scratch_shapes=[
            pltpu.VMEM((rows, cols), bf16),
            pltpu.VMEM((rows, cols), f32),
            pltpu.VMEM((rows, cols), bf16),
            pltpu.VMEM((rows, cols), bf16),
            tile(near * left_piece),
            tile(near, left_piece),
            tile(outer, left_piece),
            tile(near * left_piece),
            tile(n * small),
            tile(inner, outer * small),
            tile(outer * small),
            tile(outer, small),
            tile(n * small),
            pltpu.VMEM((2 * rank, rows), f32),
            pltpu.SemaphoreType.DMA((2, chunks)),
            pltpu.SemaphoreType.DMA((copies,)),
            pltpu.SemaphoreType.DMA((copies,)),
        ],
        compiler_params=pltpu.CompilerParams(collective_id=0, has_side_effects=True, vmem_limit_bytes=VMEM_LIMIT),
        name="reduce",
    )(grads[0], residual[0], q_prev.T)
    new, q_next, basis = pl.pallas_call(
        finish_kernel,
        out_shape=(
            jax.ShapeDtypeStruct((rows, cols), f32),
            jax.ShapeDtypeStruct((rank, cols), f32),
            jax.ShapeDtypeStruct((rank, rows), f32),
        ),
        in_specs=[vmem] * 5,
        out_specs=(hbm, hbm, vmem),
        scratch_shapes=[
            pltpu.VMEM((rows, cols), f32),
            pltpu.VMEM((rank, cols), f32),
            pltpu.SemaphoreType.DMA((2, chunks)),
        ],
        compiler_params=pltpu.CompilerParams(vmem_limit_bytes=VMEM_LIMIT),
        name="finish",
    )(merged, t_sum, b_four, w_four, basis)
    return (q_next.T, basis.T, new[None])


def solution(mesh):
    in_specs = (P("dp", None, "tensor"), P("dp", None, "tensor"), P("tensor", None))
    out_specs = (P("tensor", None), P(), P("dp", None, "tensor"))
    return jax.shard_map(local, mesh=mesh, in_specs=in_specs, out_specs=out_specs, check_vma=False)
```

```python
import functools

import jax
import jax.numpy as jnp
from jax import lax
from jax.experimental import pallas as pl
from jax.experimental.pallas import tpu as pltpu
from jax.sharding import PartitionSpec as P

MESH = pl.DeviceIdType.MESH
HIGHEST = lax.Precision.HIGHEST
SUB, LANE = 8, 128
FIRST_STEPS = 40
VMEM_LIMIT = 24 << 20


def split(x):
    hi = x.astype(jnp.bfloat16)
    lo = (x - hi.astype(jnp.float32)).astype(jnp.bfloat16)
    return hi, lo


def dot(a, b, dims=((1,), (0,)), precision=None):
    return lax.dot_general(a, b, (dims, ((), ())), precision=precision, preferred_element_type=jnp.float32)


def eliminate(tiles, start, stop, rank):
    tiles = list(tiles)
    index = lax.broadcasted_iota(jnp.int32, tiles[0].shape, 0)
    for k in range(start, stop):
        block, r = divmod(k, SUB)
        row = tiles[block][r : r + 1, :]
        scaled = row * (1.0 / row[:, k : k + 1])
        for b in range(block, rank // SUB):
            if b == block and r == SUB - 1:
                continue
            column = tiles[b][:, k : k + 1]
            if b == block:
                column = jnp.where(index[:, :1] > r, column, 0.0)
            tiles[b] = tiles[b] - column * scaled
    return tiles


def reduce_kernel(
    n, inner, outer, tensor,
    g_hbm, r_hbm, q_hbm, m_ref, t_ref, b_ref, w_ref, basis_ref,
    q_ref, g_in, r_in, m_hi, m_lo, left_own, left_in, left_mid, left_all,
    t_own, t_in, t_sum, t_in2, t_all, gram_b, sem_q, sems_load, sems_send, sems_recv,
):
    rows, cols = g_in.shape
    rank = q_ref.shape[0]
    block = 2 * LANE
    starts = range(0, cols, block)
    load_q = pltpu.make_async_copy(q_hbm, q_ref, sem_q)
    load_q.start()
    loads = []
    for j, c in enumerate(starts):
        here = pl.ds(c, block)
        pair = (
            pltpu.make_async_copy(g_hbm.at[:, here], g_in.at[:, here], sems_load.at[0, j]),
            pltpu.make_async_copy(r_hbm.at[:, here], r_in.at[:, here], sems_load.at[1, j]),
        )
        for copy in pair:
            copy.start()
        loads.append(pair)

    me_dp, me_t = lax.axis_index("dp"), lax.axis_index("tensor")
    i, o = lax.rem(me_dp, inner), lax.div(me_dp, inner)
    near = inner * tensor
    place = i * tensor + me_t

    def near_device(k):
        peer = lax.rem(place + k, near)
        return peer, (o * inner + lax.div(peer, tensor), lax.rem(peer, tensor))

    def plane_device(k):
        peer = lax.rem(i + k, inner)
        return peer, (o * inner + peer, me_t)

    def far(j):
        low = jnp.where(outer - 1 - j > o, outer - 1 - j, outer - 2 - j)
        high = jnp.where(j < o, j, j + 1)
        return jnp.where(2 * o < outer, low, high)

    def far_device(peer):
        return (peer * inner + i, me_t)

    barrier = pltpu.get_barrier_semaphore()
    for k in range(1, near):
        pl.semaphore_signal(barrier, inc=1, device_id=near_device(k)[1], device_id_type=MESH)
    for k in range(1, outer):
        pl.semaphore_signal(barrier, inc=1, device_id=far_device(lax.rem(o + k, outer)), device_id_type=MESH)

    used = [0]
    sent = []

    def slots(count):
        used[0] += count
        return used[0] - count

    def remote(src, dst, slot, device):
        return pltpu.make_async_remote_copy(
            src_ref=src, dst_ref=dst, send_sem=sems_send.at[len(sent)], recv_sem=sems_recv.at[slot],
            device_id=device, device_id_type=MESH,
        )

    def send(src, dst, slot, device):
        copy = remote(src, dst, slot, device)
        copy.start()
        sent.append(copy)
        return copy

    def landed(dst, slot):
        remote(dst, dst, slot, near_device(1)[1]).wait_recv()

    load_q.wait()
    q_hi, q_lo = split(q_ref[...])
    q_two = jnp.concatenate([q_hi, q_lo], axis=0)
    total = jnp.zeros((2 * rank, rows), jnp.float32)
    low = jnp.zeros((rank, rows), jnp.float32)
    for (load_g, load_r), c in zip(loads, starts):
        load_g.wait()
        load_r.wait()
        merged = g_in[:, c : c + block].astype(jnp.float32) + r_in[:, c : c + block]
        m_ref[:, c : c + block] = merged
        hi, lo = split(merged)
        m_hi[:, c : c + block] = hi
        m_lo[:, c : c + block] = lo
        total += dot(q_two[:, c : c + block], hi, ((1,), (1,)))
        low += dot(q_hi[:, c : c + block], lo, ((1,), (1,)))
    part = (total[:rank] + total[rank:]) + low
    tall = rank // SUB
    left_tiles = tall * (rows // LANE)
    for b in range(rows // LANE):
        left_own[b * tall : (b + 1) * tall] = part[:, b * LANE : (b + 1) * LANE].reshape(tall, SUB, LANE)
    if left_own.shape[0] > left_tiles:
        left_own[left_tiles:] = jnp.zeros((left_own.shape[0] - left_tiles, SUB, LANE), jnp.float32)
    piece = left_own.shape[0] // near

    pl.semaphore_wait(barrier, near - 1 + outer - 1)

    base = slots(near)
    copies = []
    for k in range(1, near):
        peer, device = near_device(k)
        copies.append(send(left_own.at[pl.ds(peer * piece, piece)], left_in.at[k], base + k, device))
    value = left_own[pl.ds(place * piece, piece)]
    for k, copy in enumerate(copies):
        copy.wait_recv()
        value += left_in[k + 1]
    left_mid[o] = value
    base = slots(outer)
    for j in range(outer - 1):
        send(left_mid.at[o], left_mid.at[o], base + o, far_device(far(j)))
    for j in reversed(range(outer - 1)):
        landed(left_mid.at[far(j)], base + far(j))
    value = left_mid[0]
    for k in range(1, outer):
        value += left_mid[k]
    here = left_all.at[pl.ds(place * piece, piece)]
    here[...] = value / n
    base = slots(near)
    copies = [send(here, here, base + k, near_device(k)[1]) for k in range(1, near)]
    for copy in copies:
        copy.wait_recv()
    left = jnp.concatenate(
        [left_all[b * tall : (b + 1) * tall].reshape(rank, LANE) for b in range(rows // LANE)], axis=1
    )

    l_hi, l_lo = split(left)
    l_two = jnp.concatenate([l_hi, l_lo], axis=0)
    t_tiles = tall * (cols // LANE)
    for c in starts:
        both = dot(l_two, m_hi[:, c : c + block])
        value = (both[:rank] + both[rank:]) + dot(l_hi, m_lo[:, c : c + block])
        for d in range(0, block, LANE):
            b = (c + d) // LANE
            t_own[b * tall : (b + 1) * tall] = value[:, d : d + LANE].reshape(tall, SUB, LANE)
    if t_own.shape[0] > t_tiles:
        t_own[t_tiles:] = jnp.zeros((t_own.shape[0] - t_tiles, SUB, LANE), jnp.float32)
    small = t_own.shape[0] // n
    large = small * outer

    order = [far(j) for j in range(outer - 1)] + [o]
    base = slots(outer * inner)
    steps = []
    for j, b in enumerate(order):
        copies = []
        for k in range(1, inner):
            peer, device = plane_device(k)
            copies.append(send(
                t_own.at[pl.ds(peer * large + b * small, small)], t_in.at[k, pl.ds(b * small, small)],
                base + j * inner + k, device,
            ))
        steps.append(copies)

    gram_b[:rank] = left
    gram_b[rank:] = jnp.zeros_like(left)
    gram = dot(left, gram_b[...], ((1,), (1,)), HIGHEST)
    row_id = lax.broadcasted_iota(jnp.int32, gram.shape, 0)
    lane_id = lax.broadcasted_iota(jnp.int32, gram.shape, 1)
    gram = gram + jnp.where(lane_id == row_id + rank, 1.0, 0.0)
    tiles = [gram[b : b + SUB] for b in range(0, rank, SUB)]
    middle = FIRST_STEPS * rank // 64
    tiles = eliminate(tiles, 0, middle, rank)

    base = slots(outer)
    for copies, b in zip(steps, order):
        mine = t_own[pl.ds(i * large + b * small, small)]
        for k, copy in enumerate(copies):
            copy.wait_recv()
            mine += t_in[k + 1, pl.ds(b * small, small)]
        there = t_sum.at[pl.ds(b * small, small)]
        there[...] = mine
        if copies is not steps[-1]:
            send(there, t_in2.at[o], base + o, far_device(b))

    tiles = eliminate(tiles, middle, rank, rank)

    mine = t_sum[pl.ds(o * small, small)]
    for b in order[:-1]:
        landed(t_in2.at[b], base + b)
        mine += t_in2[b]
    here = t_all.at[pl.ds(i * large + o * small, small)]
    here[...] = mine
    base = slots(outer)
    for b in order[:-1]:
        send(here, here, base + o, far_device(b))
    last = slots(inner * outer)

    def spread(b):
        part = t_all.at[pl.ds(i * large + b * small, small)]
        for k in range(1, inner):
            send(part, part, last + k * outer + b, plane_device(k)[1])

    spread(o)

    done = jnp.concatenate(tiles, axis=0)
    pivot = jnp.sum(jnp.where(lane_id == row_id, done, 0.0), axis=1, keepdims=True)
    done = done * (1.0 / jnp.sqrt(pivot))
    w_two = jnp.where(lane_id < rank, pltpu.roll(done, rank, 1), done)
    basis = dot(w_two[:, :rank], left, precision=HIGHEST)
    basis_ref[...] = basis
    w_hi, w_lo = split(w_two / n)
    w_ref[...] = jnp.concatenate([w_hi, w_lo], axis=1)

    for b in reversed(order[:-1]):
        landed(t_all.at[pl.ds(i * large + b * small, small)], base + b)
        spread(b)

    b_hi, b_lo = split(jnp.concatenate([basis, basis], axis=0).T)
    b_ref[...] = jnp.concatenate([b_hi, b_lo], axis=1)

    for b in range(outer):
        for k in range(1, inner):
            peer = lax.rem(i + inner - k, inner)
            landed(t_all.at[pl.ds(peer * large + b * small, small)], last + k * outer + b)
    t_ref[...] = t_all[:t_tiles]
    for copy in sent:
        copy.wait_send()


def finish_kernel(
    m_ref, t_ref, b_ref, w_ref, basis_ref, new_hbm, next_hbm, out_basis_ref,
    new_out, next_out, sems_store,
):
    rank, cols = next_out.shape
    tall = rank // SUB
    block = 2 * LANE
    out_basis_ref[...] = basis_ref[...]
    stores = []
    for j, c in enumerate(range(0, cols, block)):
        here = pl.ds(c, block)
        t = jnp.concatenate(
            [t_ref[b * tall : (b + 1) * tall].reshape(rank, LANE) for b in range(c // LANE, (c + block) // LANE)],
            axis=1,
        )
        t_hi, t_lo = split(t)
        q_next = dot(w_ref[...], jnp.concatenate([t_hi, t_lo, t_hi, t_lo], axis=0))
        next_out[:, c : c + block] = q_next
        stores.append(pltpu.make_async_copy(next_out.at[:, here], next_hbm.at[:, here], sems_store.at[0, j]))
        stores[-1].start()
        n_hi, n_lo = split(q_next)
        update = dot(b_ref[...], jnp.concatenate([n_hi, n_lo, n_hi, n_lo], axis=0))
        new_out[:, c : c + block] = m_ref[:, c : c + block] - update
        stores.append(pltpu.make_async_copy(new_out.at[:, here], new_hbm.at[:, here], sems_store.at[1, j]))
        stores[-1].start()
    for copy in stores:
        copy.wait()


def local(grads, residual, q_prev):
    n, tensor = lax.axis_size("dp"), lax.axis_size("tensor")
    inner = max(d for d in range(1, n + 1) if n % d == 0 and d * d <= n)
    outer = n // inner
    rows, cols = grads.shape[1:]
    rank = q_prev.shape[1]
    near = inner * tensor
    t_tiles = (rank // SUB) * (cols // LANE)
    left_piece = pl.cdiv((rank // SUB) * (rows // LANE), near)
    small = pl.cdiv(t_tiles, n)
    copies = 2 * near + 4 * outer + 2 * inner * outer
    f32, bf16 = jnp.float32, jnp.bfloat16
    tile = lambda *dims: pltpu.VMEM((*dims, SUB, LANE), f32)
    vmem = pl.BlockSpec(memory_space=pltpu.VMEM)
    hbm = pl.BlockSpec(memory_space=pltpu.HBM)
    chunks = cols // (2 * LANE)
    merged, t_sum, b_four, w_four, basis = pl.pallas_call(
        functools.partial(reduce_kernel, n, inner, outer, tensor),
        out_shape=(
            jax.ShapeDtypeStruct((rows, cols), f32),
            jax.ShapeDtypeStruct((t_tiles, SUB, LANE), f32),
            jax.ShapeDtypeStruct((rows, 4 * rank), bf16),
            jax.ShapeDtypeStruct((rank, 4 * rank), bf16),
            jax.ShapeDtypeStruct((rank, rows), f32),
        ),
        in_specs=[hbm] * 3,
        out_specs=(vmem,) * 5,
        scratch_shapes=[
            pltpu.VMEM((rank, cols), f32),
            pltpu.VMEM((rows, cols), bf16),
            pltpu.VMEM((rows, cols), f32),
            pltpu.VMEM((rows, cols), bf16),
            pltpu.VMEM((rows, cols), bf16),
            tile(near * left_piece),
            tile(near, left_piece),
            tile(outer, left_piece),
            tile(near * left_piece),
            tile(n * small),
            tile(inner, outer * small),
            tile(outer * small),
            tile(outer, small),
            tile(n * small),
            pltpu.VMEM((2 * rank, rows), f32),
            pltpu.SemaphoreType.DMA,
            pltpu.SemaphoreType.DMA((2, chunks)),
            pltpu.SemaphoreType.DMA((copies,)),
            pltpu.SemaphoreType.DMA((copies,)),
        ],
        compiler_params=pltpu.CompilerParams(collective_id=0, has_side_effects=True, vmem_limit_bytes=VMEM_LIMIT),
        name="reduce",
    )(*(pltpu.with_memory_space_constraint(x, pltpu.HBM) for x in (grads[0], residual[0], q_prev.T)))
    new, q_next, basis = pl.pallas_call(
        finish_kernel,
        out_shape=(
            jax.ShapeDtypeStruct((rows, cols), f32),
            jax.ShapeDtypeStruct((rank, cols), f32),
            jax.ShapeDtypeStruct((rank, rows), f32),
        ),
        in_specs=[vmem] * 5,
        out_specs=(hbm, hbm, vmem),
        scratch_shapes=[
            pltpu.VMEM((rows, cols), f32),
            pltpu.VMEM((rank, cols), f32),
            pltpu.SemaphoreType.DMA((2, chunks)),
        ],
        compiler_params=pltpu.CompilerParams(vmem_limit_bytes=VMEM_LIMIT),
        name="finish",
    )(merged, t_sum, b_four, w_four, basis)
    return (q_next.T, basis.T, new[None])


def solution(mesh):
    in_specs = (P("dp", None, "tensor"), P("dp", None, "tensor"), P("tensor", None))
    out_specs = (P("tensor", None), P(), P("dp", None, "tensor"))
    return jax.shard_map(local, mesh=mesh, in_specs=in_specs, out_specs=out_specs, check_vma=False)
```

```python
import functools

import jax
import jax.numpy as jnp
from jax import lax
from jax.experimental import pallas as pl
from jax.experimental.pallas import tpu as pltpu
from jax.sharding import PartitionSpec as P

MESH = pl.DeviceIdType.MESH
HIGHEST = lax.Precision.HIGHEST
SUB, LANE = 8, 128
FIRST_STEPS = 40
VMEM_LIMIT = 24 << 20


def columns_at_once(cols):
    return cols // 2 if cols % (2 * LANE) == 0 else LANE


def split(x):
    hi = x.astype(jnp.bfloat16)
    lo = (x - hi.astype(jnp.float32)).astype(jnp.bfloat16)
    return hi, lo


def dot(a, b, dims=((1,), (0,)), precision=None):
    return lax.dot_general(a, b, (dims, ((), ())), precision=precision, preferred_element_type=jnp.float32)


def eliminate(tiles, start, stop, rank):
    tiles = list(tiles)
    index = lax.broadcasted_iota(jnp.int32, tiles[0].shape, 0)
    for k in range(start, stop):
        block, r = divmod(k, SUB)
        row = tiles[block][r : r + 1, :]
        scaled = row * (1.0 / row[:, k : k + 1])
        for b in range(block, rank // SUB):
            if b == block and r == SUB - 1:
                continue
            column = tiles[b][:, k : k + 1]
            if b == block:
                column = jnp.where(index[:, :1] > r, column, 0.0)
            tiles[b] = tiles[b] - column * scaled
    return tiles


def reduce_kernel(
    n, inner, outer, tensor,
    g_hbm, r_hbm, q_hbm, m_ref, t_ref, b_ref, w_ref, basis_ref,
    q_ref, g_in, r_in, m_hi, m_lo, left_own, left_in, left_mid, left_all,
    t_own, t_in, t_sum, t_in2, t_all, gram_b, sem_q, sems_load, sems_send, sems_recv,
):
    rows, cols = g_in.shape
    rank = q_ref.shape[0]
    block = columns_at_once(cols)
    starts = range(0, cols, block)
    load_q = pltpu.make_async_copy(q_hbm, q_ref, sem_q)
    load_q.start()
    loads = []
    for j, c in enumerate(starts):
        here = pl.ds(c, block)
        pair = (
            pltpu.make_async_copy(g_hbm.at[:, here], g_in.at[:, here], sems_load.at[0, j]),
            pltpu.make_async_copy(r_hbm.at[:, here], r_in.at[:, here], sems_load.at[1, j]),
        )
        for copy in pair:
            copy.start()
        loads.append(pair)

    me_dp, me_t = lax.axis_index("dp"), lax.axis_index("tensor")
    i, o = lax.rem(me_dp, inner), lax.div(me_dp, inner)
    near = inner * tensor
    place = i * tensor + me_t

    def near_device(k):
        peer = lax.rem(place + k, near)
        return peer, (o * inner + lax.div(peer, tensor), lax.rem(peer, tensor))

    def plane_device(k):
        peer = lax.rem(i + k, inner)
        return peer, (o * inner + peer, me_t)

    def far(j):
        low = jnp.where(outer - 1 - j > o, outer - 1 - j, outer - 2 - j)
        high = jnp.where(j < o, j, j + 1)
        return jnp.where(2 * o < outer, low, high)

    def far_device(peer):
        return (peer * inner + i, me_t)

    barrier = pltpu.get_barrier_semaphore()
    for k in range(1, near):
        pl.semaphore_signal(barrier, inc=1, device_id=near_device(k)[1], device_id_type=MESH)
    for k in range(1, outer):
        pl.semaphore_signal(barrier, inc=1, device_id=far_device(lax.rem(o + k, outer)), device_id_type=MESH)

    used = [0]
    sent = []

    def slots(count):
        used[0] += count
        return used[0] - count

    def remote(src, dst, slot, device):
        return pltpu.make_async_remote_copy(
            src_ref=src, dst_ref=dst, send_sem=sems_send.at[len(sent)], recv_sem=sems_recv.at[slot],
            device_id=device, device_id_type=MESH,
        )

    def send(src, dst, slot, device):
        copy = remote(src, dst, slot, device)
        copy.start()
        sent.append(copy)
        return copy

    def landed(dst, slot):
        remote(dst, dst, slot, near_device(1)[1]).wait_recv()

    load_q.wait()
    q_hi, q_lo = split(q_ref[...])
    q_two = jnp.concatenate([q_hi, q_lo], axis=0)
    total = jnp.zeros((2 * rank, rows), jnp.float32)
    low = jnp.zeros((rank, rows), jnp.float32)
    for (load_g, load_r), c in zip(loads, starts):
        load_g.wait()
        load_r.wait()
        merged = g_in[:, c : c + block].astype(jnp.float32) + r_in[:, c : c + block]
        m_ref[:, c : c + block] = merged
        hi, lo = split(merged)
        m_hi[:, c : c + block] = hi
        m_lo[:, c : c + block] = lo
        total += dot(q_two[:, c : c + block], hi, ((1,), (1,)))
        low += dot(q_hi[:, c : c + block], lo, ((1,), (1,)))
    part = (total[:rank] + total[rank:]) + low
    tall = rank // SUB
    left_tiles = tall * (rows // LANE)
    for b in range(rows // LANE):
        left_own[b * tall : (b + 1) * tall] = part[:, b * LANE : (b + 1) * LANE].reshape(tall, SUB, LANE)
    if left_own.shape[0] > left_tiles:
        left_own[left_tiles:] = jnp.zeros((left_own.shape[0] - left_tiles, SUB, LANE), jnp.float32)
    piece = left_own.shape[0] // near

    pl.semaphore_wait(barrier, near - 1 + outer - 1)

    base = slots(near)
    copies = []
    for k in range(1, near):
        peer, device = near_device(k)
        copies.append(send(left_own.at[pl.ds(peer * piece, piece)], left_in.at[k], base + k, device))
    value = left_own[pl.ds(place * piece, piece)]
    for k, copy in enumerate(copies):
        copy.wait_recv()
        value += left_in[k + 1]
    left_mid[o] = value
    base = slots(outer)
    for j in range(outer - 1):
        send(left_mid.at[o], left_mid.at[o], base + o, far_device(far(j)))
    for j in reversed(range(outer - 1)):
        landed(left_mid.at[far(j)], base + far(j))
    value = left_mid[0]
    for k in range(1, outer):
        value += left_mid[k]
    here = left_all.at[pl.ds(place * piece, piece)]
    here[...] = value / n
    base = slots(near)
    copies = [send(here, here, base + k, near_device(k)[1]) for k in range(1, near)]
    for copy in copies:
        copy.wait_recv()
    left = jnp.concatenate(
        [left_all[b * tall : (b + 1) * tall].reshape(rank, LANE) for b in range(rows // LANE)], axis=1
    )

    l_hi, l_lo = split(left)
    l_two = jnp.concatenate([l_hi, l_lo], axis=0)
    t_tiles = tall * (cols // LANE)
    for c in starts:
        both = dot(l_two, m_hi[:, c : c + block])
        value = (both[:rank] + both[rank:]) + dot(l_hi, m_lo[:, c : c + block])
        for d in range(0, block, LANE):
            b = (c + d) // LANE
            t_own[b * tall : (b + 1) * tall] = value[:, d : d + LANE].reshape(tall, SUB, LANE)
    if t_own.shape[0] > t_tiles:
        t_own[t_tiles:] = jnp.zeros((t_own.shape[0] - t_tiles, SUB, LANE), jnp.float32)
    small = t_own.shape[0] // n
    large = small * outer

    order = [far(j) for j in range(outer - 1)] + [o]
    base = slots(outer * inner)
    steps = []
    for j, b in enumerate(order):
        copies = []
        for k in range(1, inner):
            peer, device = plane_device(k)
            copies.append(send(
                t_own.at[pl.ds(peer * large + b * small, small)], t_in.at[k, pl.ds(b * small, small)],
                base + j * inner + k, device,
            ))
        steps.append(copies)

    gram_b[:rank] = left
    gram_b[rank:] = jnp.zeros_like(left)
    gram = dot(left, gram_b[...], ((1,), (1,)), HIGHEST)
    row_id = lax.broadcasted_iota(jnp.int32, gram.shape, 0)
    lane_id = lax.broadcasted_iota(jnp.int32, gram.shape, 1)
    gram = gram + jnp.where(lane_id == row_id + rank, 1.0, 0.0)
    tiles = [gram[b : b + SUB] for b in range(0, rank, SUB)]
    middle = FIRST_STEPS * rank // 64
    tiles = eliminate(tiles, 0, middle, rank)

    base = slots(outer)
    for copies, b in zip(steps, order):
        mine = t_own[pl.ds(i * large + b * small, small)]
        for k, copy in enumerate(copies):
            copy.wait_recv()
            mine += t_in[k + 1, pl.ds(b * small, small)]
        there = t_sum.at[pl.ds(b * small, small)]
        there[...] = mine
        if copies is not steps[-1]:
            send(there, t_in2.at[o], base + o, far_device(b))

    tiles = eliminate(tiles, middle, rank, rank)

    mine = t_sum[pl.ds(o * small, small)]
    for b in order[:-1]:
        landed(t_in2.at[b], base + b)
        mine += t_in2[b]
    here = t_all.at[pl.ds(i * large + o * small, small)]
    here[...] = mine
    base = slots(outer)
    for b in order[:-1]:
        send(here, here, base + o, far_device(b))
    last = slots(inner * outer)

    def spread(b):
        part = t_all.at[pl.ds(i * large + b * small, small)]
        for k in range(1, inner):
            send(part, part, last + k * outer + b, plane_device(k)[1])

    spread(o)

    done = jnp.concatenate(tiles, axis=0)
    pivot = jnp.sum(jnp.where(lane_id == row_id, done, 0.0), axis=1, keepdims=True)
    done = done * (1.0 / jnp.sqrt(pivot))
    w_two = jnp.where(lane_id < rank, pltpu.roll(done, rank, 1), done)
    basis = dot(w_two[:, :rank], left, precision=HIGHEST)
    basis_ref[...] = basis
    w_hi, w_lo = split(w_two / n)
    w_ref[...] = jnp.concatenate([w_hi, w_lo], axis=1)

    for b in reversed(order[:-1]):
        landed(t_all.at[pl.ds(i * large + b * small, small)], base + b)
        spread(b)

    b_hi, b_lo = split(jnp.concatenate([basis, basis], axis=0).T)
    b_ref[...] = jnp.concatenate([b_hi, b_lo], axis=1)

    for b in range(outer):
        for k in range(1, inner):
            peer = lax.rem(i + inner - k, inner)
            landed(t_all.at[pl.ds(peer * large + b * small, small)], last + k * outer + b)
    t_ref[...] = t_all[:t_tiles]
    for copy in sent:
        copy.wait_send()


def finish_kernel(
    m_ref, t_ref, b_ref, w_ref, basis_ref, new_hbm, next_hbm, out_basis_ref,
    new_out, next_out, sems_store,
):
    rank, cols = next_out.shape
    tall = rank // SUB
    block = columns_at_once(cols)
    out_basis_ref[...] = basis_ref[...]
    stores = []
    for j, c in enumerate(range(0, cols, block)):
        here = pl.ds(c, block)
        t = jnp.concatenate(
            [t_ref[b * tall : (b + 1) * tall].reshape(rank, LANE) for b in range(c // LANE, (c + block) // LANE)],
            axis=1,
        )
        t_hi, t_lo = split(t)
        q_next = dot(w_ref[...], jnp.concatenate([t_hi, t_lo, t_hi, t_lo], axis=0))
        next_out[:, c : c + block] = q_next
        stores.append(pltpu.make_async_copy(next_out.at[:, here], next_hbm.at[:, here], sems_store.at[0, j]))
        stores[-1].start()
        n_hi, n_lo = split(q_next)
        update = dot(b_ref[...], jnp.concatenate([n_hi, n_lo, n_hi, n_lo], axis=0))
        new_out[:, c : c + block] = m_ref[:, c : c + block] - update
        stores.append(pltpu.make_async_copy(new_out.at[:, here], new_hbm.at[:, here], sems_store.at[1, j]))
        stores[-1].start()
    for copy in stores:
        copy.wait()


def local(grads, residual, q_prev):
    n, tensor = lax.axis_size("dp"), lax.axis_size("tensor")
    inner = max(d for d in range(1, n + 1) if n % d == 0 and d * d <= n)
    outer = n // inner
    rows, cols = grads.shape[1:]
    rank = q_prev.shape[1]
    near = inner * tensor
    t_tiles = (rank // SUB) * (cols // LANE)
    left_piece = pl.cdiv((rank // SUB) * (rows // LANE), near)
    small = pl.cdiv(t_tiles, n)
    copies = 2 * near + 4 * outer + 2 * inner * outer
    f32, bf16 = jnp.float32, jnp.bfloat16
    tile = lambda *dims: pltpu.VMEM((*dims, SUB, LANE), f32)
    vmem = pl.BlockSpec(memory_space=pltpu.VMEM)
    hbm = pl.BlockSpec(memory_space=pltpu.HBM)
    chunks = cols // columns_at_once(cols)
    merged, t_sum, b_four, w_four, basis = pl.pallas_call(
        functools.partial(reduce_kernel, n, inner, outer, tensor),
        out_shape=(
            jax.ShapeDtypeStruct((rows, cols), f32),
            jax.ShapeDtypeStruct((t_tiles, SUB, LANE), f32),
            jax.ShapeDtypeStruct((rows, 4 * rank), bf16),
            jax.ShapeDtypeStruct((rank, 4 * rank), bf16),
            jax.ShapeDtypeStruct((rank, rows), f32),
        ),
        in_specs=[hbm] * 3,
        out_specs=(vmem,) * 5,
        scratch_shapes=[
            pltpu.VMEM((rank, cols), f32),
            pltpu.VMEM((rows, cols), bf16),
            pltpu.VMEM((rows, cols), f32),
            pltpu.VMEM((rows, cols), bf16),
            pltpu.VMEM((rows, cols), bf16),
            tile(near * left_piece),
            tile(near, left_piece),
            tile(outer, left_piece),
            tile(near * left_piece),
            tile(n * small),
            tile(inner, outer * small),
            tile(outer * small),
            tile(outer, small),
            tile(n * small),
            pltpu.VMEM((2 * rank, rows), f32),
            pltpu.SemaphoreType.DMA,
            pltpu.SemaphoreType.DMA((2, chunks)),
            pltpu.SemaphoreType.DMA((copies,)),
            pltpu.SemaphoreType.DMA((copies,)),
        ],
        compiler_params=pltpu.CompilerParams(collective_id=0, has_side_effects=True, vmem_limit_bytes=VMEM_LIMIT),
        name="reduce",
    )(*(pltpu.with_memory_space_constraint(x, pltpu.HBM) for x in (grads[0], residual[0], q_prev.T)))
    new, q_next, basis = pl.pallas_call(
        finish_kernel,
        out_shape=(
            jax.ShapeDtypeStruct((rows, cols), f32),
            jax.ShapeDtypeStruct((rank, cols), f32),
            jax.ShapeDtypeStruct((rank, rows), f32),
        ),
        in_specs=[vmem] * 5,
        out_specs=(hbm, hbm, vmem),
        scratch_shapes=[
            pltpu.VMEM((rows, cols), f32),
            pltpu.VMEM((rank, cols), f32),
            pltpu.SemaphoreType.DMA((2, chunks)),
        ],
        compiler_params=pltpu.CompilerParams(vmem_limit_bytes=VMEM_LIMIT),
        name="finish",
    )(merged, t_sum, b_four, w_four, basis)
    return (q_next.T, basis.T, new[None])


def solution(mesh):
    in_specs = (P("dp", None, "tensor"), P("dp", None, "tensor"), P("tensor", None))
    out_specs = (P("tensor", None), P(), P("dp", None, "tensor"))
    return jax.shard_map(local, mesh=mesh, in_specs=in_specs, out_specs=out_specs, check_vma=False)
```
